32 devices in a mesh: groups: 2 (over y), dp: 4 (over z), layer: 4 (over x, core).
Axes of the slice: x: 2, y: 2, z: 4, core: 2. Of those that a mesh axis runs over, the one named last changes fastest.
Arguments:
- layer_inputs: float32 [4, 1024, 512], P('layer', ('groups', 'dp')), parts along dimension 1, may hold values from -6 to 6
- pre_acts: float32 [4, 1024, 512], P('layer', ('groups', 'dp')), parts along dimension 1, may hold values from -6 to 6
- layer_outputs: float32 [4, 1024, 512], P('layer', ('groups', 'dp')), parts along dimension 1, may hold values from -6 to 6
- multipliers: float32 [4, 1024, 512], P('layer', ('groups', 'dp')), parts along dimension 1, may hold values from -6 to 6
- weights: float32 [8, 512, 512], P(('groups', 'layer')), parts along dimension 0, may hold values from -0.25 to 0.25
- biases: float32 [8, 512], P(('groups', 'layer')), parts along dimension 0, may hold values from -3 to 3
- prev_outputs: float32 [1024, 512], P(('groups', 'dp')), parts along dimension 0, may hold values from -6 to 6
- prev_multipliers: float32 [1024, 512], P(('groups', 'dp')), parts along dimension 0, may hold values from -6 to 6
- next_inputs: float32 [1024, 512], P(('groups', 'dp')), parts along dimension 0, may hold values from -6 to 6
- row_order: int32 [8, 128], P(('groups', 'dp')), parts along dimension 0, may hold values from 0 to 127, each once within a row
Outputs:
- new_inputs: float32 [4, 1024, 512], P('layer', ('groups', 'dp')), parts along dimension 1
- new_preacts: float32 [4, 1024, 512], P('layer', ('groups', 'dp')), parts along dimension 1
- new_outputs: float32 [4, 1024, 512], P('layer', ('groups', 'dp')), parts along dimension 1
- new_multipliers: float32 [4, 1024, 512], P('layer', ('groups', 'dp')), parts along dimension 1
- new_weights: float32 [8, 512, 512], P(('groups', 'layer')), parts along dimension 0
- new_biases: float32 [8, 512], P(('groups', 'layer')), parts along dimension 0
The draws below stay inside these ranges and needn't reach their ends.
There are 2 independent parts, one for each index of `groups`. The reference program is written for one: setup_inputs(seed, part) draws one part's arguments, and reference() takes and returns one part's arrays. A program takes and returns all parts, laid end to end along the dimension named above; each array names one. Nothing has to cross between parts.
Inputs may be any that keep to these rules, and one draw needn't show every extreme that they name: Each row of row_order holds every number of 0 to 127 once.
All inputs are finite; a program needn't handle non-finite values.
Results may differ from the reference program's by a relative error of at most 0.0001.
Values sent between devices are 32-bit elements; how exact they have to be, the bound alone decides.
A program may use at most 64 MiB of HBM per device.

```python
import jax
import jax.numpy as jnp
from jax import lax

D = 512
ROWS = 128
INNER = 3
PASSES = 1
NODES = 512
LAYERS = 4
N_DP = 4


def block_scale(stream_key, extent, cuts, least, largest):
    loudness = 1.0
    for position, shards_of in cuts:
        draws = jax.random.uniform(jax.random.fold_in(jax.random.fold_in(stream_key, 6), position), (shards_of,), jnp.float32, least / len(cuts), largest / len(cuts))
        loudness = loudness * jnp.repeat(jnp.exp(draws), extent[position] // shards_of).reshape((-1,) + (1,) * (len(extent) - 1 - position))
    return loudness


def gaussian(stream_key, shape, width, most, cuts=(), held_as=jnp.bfloat16):
    values = width * jax.random.normal(stream_key, shape, jnp.float32)
    if cuts:
        values = values * block_scale(stream_key, shape, cuts, -0.22, 0.18)
    return jnp.clip(values, -most, most).astype(held_as)


def setup_inputs(seed: int = 0, part: int = 0) -> dict:
    key_of = jax.random.split(jax.random.key(seed), 11)
    part_splits = jax.random.split(jax.random.fold_in(key_of[10], part), 11)
    return {
        "layer_inputs": gaussian(part_splits[0], (LAYERS, NODES, D), 1.0, 6.0, ((0, 4), (1, 4)), jnp.float32),
        "pre_acts": gaussian(part_splits[1], (LAYERS, NODES, D), 1.0, 6.0, ((0, 4), (1, 4)), jnp.float32),
        "layer_outputs": gaussian(part_splits[2], (LAYERS, NODES, D), 1.0, 6.0, ((0, 4), (1, 4)), jnp.float32),
        "multipliers": gaussian(part_splits[3], (LAYERS, NODES, D), 1.0, 6.0, ((0, 4), (1, 4)), jnp.float32),
        "weights": gaussian(part_splits[4], (LAYERS, D, D), D ** -0.5, 0.25, ((0, 4),), jnp.float32),
        "biases": gaussian(part_splits[5], (LAYERS, D), 0.5, 3.0, ((0, 4),), jnp.float32),
        "prev_outputs": gaussian(part_splits[6], (NODES, D), 1.0, 6.0, ((0, 4),), jnp.float32),
        "prev_multipliers": gaussian(part_splits[7], (NODES, D), 1.0, 6.0, ((0, 4),), jnp.float32),
        "next_inputs": gaussian(part_splits[8], (NODES, D), 1.0, 6.0, ((0, 4),), jnp.float32),
        "row_order": jax.vmap(lambda own: jax.random.permutation(own, ROWS))(jax.random.split(part_splits[9], N_DP)).reshape((N_DP, ROWS)).astype(jnp.int32),
    }


penalty_nu = 1.0
penalty_rho = 1.0
step_input = 0.2
step_weight = 0.3
step_preact = 0.5


def matmul(form, left, right):
    return jnp.einsum(form, left, right, precision=lax.Precision.HIGHEST)


def reference(layer_inputs, pre_acts, layer_outputs, multipliers, weights, biases, prev_outputs, prev_multipliers, next_inputs, row_order):
    blocks = row_order.shape[0]
    base = (jnp.arange(blocks, dtype=jnp.int32) * ROWS)[:, None]
    gathered = (row_order.astype(jnp.int32) + base).reshape(-1)
    edge_outputs = jnp.take(prev_outputs, gathered, axis=0)
    edge_duals = jnp.take(prev_multipliers, gathered, axis=0)
    edge_inputs = jnp.take(next_inputs, gathered, axis=0)
    row_count = layer_inputs.shape[1]
    inputs, preact, outputs, duals = layer_inputs, pre_acts, layer_outputs, multipliers
    weight, offset = weights, biases
    for outer_pass in range(PASSES):
        before_out = jnp.concatenate([edge_outputs[None], outputs[:-1]], axis=0)
        before_dual = jnp.concatenate([edge_duals[None], duals[:-1]], axis=0)
        residual = matmul("lmd,lde->lme", inputs, weight) + offset[:, None, :] - preact
        back = matmul("lme,lde->lmd", residual, weight)
        inputs = inputs - step_input * (penalty_nu * back + before_dual + penalty_rho * (inputs - before_out))
        for inner_step in range(INNER):
            residual = matmul("lmd,lde->lme", inputs, weight) + offset[:, None, :] - preact
            grad_weight = matmul("lmd,lme->lde", inputs, residual)
            grad_offset = jnp.sum(residual, axis=1)
            weight = weight - (step_weight / row_count) * grad_weight
            offset = offset - (step_weight / row_count) * grad_offset
        target = matmul("lmd,lde->lme", inputs, weight) + offset[:, None, :]
        preact = preact - step_preact * ((preact - target) + (jax.nn.softplus(preact) - outputs) * jax.nn.sigmoid(preact))
        after_in = jnp.concatenate([inputs[1:], edge_inputs[None]], axis=0)
        outputs = (penalty_nu * jax.nn.softplus(preact) + duals + penalty_rho * after_in) / (penalty_nu + penalty_rho)
        duals = duals + penalty_rho * (after_in - outputs)
    return inputs, preact, outputs, duals, weight, offset
```

```python
import functools

import jax
import jax.numpy as jnp
from jax import lax
from jax.experimental import pallas as pl
from jax.experimental.pallas import tpu as pltpu
from jax.sharding import PartitionSpec as P

INNER = 3


penalty_nu = 1.0
penalty_rho = 1.0
step_input = 0.2
step_weight = 0.3
step_preact = 0.5


def from_behind(x, axis, by):
    count = lax.axis_size(axis)
    pairs = [(i, i + by) for i in range(count) if 0 <= i + by < count]
    return lax.ppermute(x, axis, pairs)


def matmul(left, right):
    return jnp.dot(left, right, precision=lax.Precision.HIGHEST)


def summed_body(
    layer_inputs,
    pre_acts,
    layer_outputs,
    multipliers,
    weights,
    biases,
    prev_outputs,
    prev_multipliers,
    next_inputs,
    row_order,
):
    row_perm = row_order[0]
    edge_outputs = jnp.take(prev_outputs, row_perm, axis=0)
    edge_duals = jnp.take(prev_multipliers, row_perm, axis=0)
    edge_inputs = jnp.take(next_inputs, row_perm, axis=0)
    first_layer = lax.axis_index("layer") == 0
    last_layer = lax.axis_index("layer") == lax.axis_size("layer") - 1
    row_count = layer_inputs.shape[1] * lax.axis_size("dp")
    scale = step_weight / row_count
    inputs, preact, outputs, duals = (
        layer_inputs[0],
        pre_acts[0],
        layer_outputs[0],
        multipliers[0],
    )
    weight, offset = (weights[0], biases[0])
    before_out, before_dual = from_behind((outputs, duals), "layer", 1)
    before_out = jnp.where(first_layer, edge_outputs, before_out)
    before_dual = jnp.where(first_layer, edge_duals, before_dual)
    coupling = before_dual + penalty_rho * (inputs - before_out)
    residual = matmul(inputs, weight) + offset[None, :] - preact
    inputs = inputs - step_input * (penalty_nu * matmul(residual, weight.T) + coupling)
    gram_matrix, cross_term, column_sums, preact_sums = lax.psum(
        (
            matmul(inputs.T, inputs),
            matmul(inputs.T, preact),
            jnp.sum(inputs, axis=0),
            jnp.sum(preact, axis=0),
        ),
        "dp",
    )
    for inner_step in range(INNER):
        grad_weight = (
            matmul(gram_matrix, weight) + column_sums[:, None] * offset[None, :] - cross_term
        )
        grad_offset = matmul(column_sums[None, :], weight)[0] + row_count * offset - preact_sums
        weight = weight - scale * grad_weight
        offset = offset - scale * grad_offset
    target = matmul(inputs, weight) + offset[None, :]
    preact = preact - step_preact * (
        preact - target + (jax.nn.softplus(preact) - outputs) * jax.nn.sigmoid(preact)
    )
    after_in = from_behind(inputs, "layer", -1)
    after_in = jnp.where(last_layer, edge_inputs, after_in)
    outputs = (penalty_nu * jax.nn.softplus(preact) + duals + penalty_rho * after_in) / (
        penalty_nu + penalty_rho
    )
    duals = duals + penalty_rho * (after_in - outputs)
    return (inputs[None], preact[None], outputs[None], duals[None], weight[None], offset[None])


MESH = pl.DeviceIdType.MESH
NN = (((1,), (0,)), ((), ()))
NT = (((1,), (1,)), ((), ()))


def split(x):
    high = x.astype(jnp.bfloat16)
    return high, (x - high.astype(jnp.float32)).astype(jnp.bfloat16)


def dot3(left, right, dims=NN):
    def one(a, b):
        return lax.dot_general(a, b, dims, preferred_element_type=jnp.float32)

    return one(left[0], right[0]) + (one(left[0], right[1]) + one(left[1], right[0]))


def softplus(v):
    return jnp.maximum(v, 0.0) + jnp.log1p(jnp.exp(-jnp.abs(v)))


def permuted(order, x):
    rows = x.shape[0]
    stored = lax.broadcasted_iota(jnp.int32, (rows, rows), 0)
    pick = jnp.where(stored == order, 1.0, 0.0).T.astype(jnp.bfloat16)
    high, rest = split(x)
    rest = x - high.astype(jnp.float32)
    mid, low = split(rest)

    def one(part):
        return jnp.dot(pick, part, preferred_element_type=jnp.float32)

    return one(high) + (one(mid) + one(low))


def kernel(
    n, layers,
    p_ref, z_ref, q_ref, u_ref, w_ref, b_ref, qb_ref, ub_ref, pb_ref, order_ref,
    p_out, z_out, q_out, u_out, w_out, b_out,
    p_all, z_all, coupling, p_next, own_coupling, w_hi, w_lo, p_hi, p_lo, pt_hi, pt_lo, target0, t_hi, t_lo, change,
    z_right, z_left, z_recv, p_right, p_left, p_recv, layer_send, layer_recv,
):
    rows, width = p_ref.shape
    total = rows * n
    me, layer = lax.axis_index("dp"), lax.axis_index("layer")
    scale = step_weight / total
    has_left, has_right = me > 0, me < n - 1
    has_below, has_above = layer > 0, layer < layers - 1

    barrier = pltpu.get_barrier_semaphore()
    for there, axis, index in (
        (has_left, "dp", me - 1), (has_right, "dp", me + 1),
        (has_below, "layer", layer - 1), (has_above, "layer", layer + 1),
    ):
        @pl.when(there)
        def _():
            pl.semaphore_signal(barrier, inc=1, device_id={axis: index}, device_id_type=MESH)

    own_coupling[...] = u_ref[...] - q_ref[...]
    w = w_ref[...]
    w_hi[...], w_lo[...] = split(w)
    ends = [jnp.where(there, 1, 0) for there in (has_left, has_right, has_below, has_above)]
    pl.semaphore_wait(barrier, ends[0] + ends[1] + ends[2] + ends[3])

    def z_copy(owner, to_right, own=False):
        return pltpu.make_async_remote_copy(
            src_ref=z_ref if own else z_all.at[owner], dst_ref=z_all.at[owner],
            send_sem=(z_right if to_right else z_left).at[owner], recv_sem=z_recv.at[owner],
            device_id={"dp": me + 1 if to_right else me - 1}, device_id_type=MESH,
        )

    def p_copy(owner, to_right):
        return pltpu.make_async_remote_copy(
            src_ref=p_all.at[owner], dst_ref=p_all.at[owner],
            send_sem=(p_right if to_right else p_left).at[owner], recv_sem=p_recv.at[owner],
            device_id={"dp": me + 1 if to_right else me - 1}, device_id_type=MESH,
        )

    up = pltpu.make_async_remote_copy(
        src_ref=own_coupling, dst_ref=coupling, send_sem=layer_send.at[0], recv_sem=layer_recv.at[0],
        device_id={"layer": layer + 1}, device_id_type=MESH,
    )
    down = pltpu.make_async_remote_copy(
        src_ref=p_all.at[me], dst_ref=p_next, send_sem=layer_send.at[1], recv_sem=layer_recv.at[1],
        device_id={"layer": layer - 1}, device_id_type=MESH,
    )

    pl.when(has_above)(lambda: up.start())
    pl.when(has_right)(lambda: z_copy(me, True, True).start())
    pl.when(has_left)(lambda: z_copy(me, False, True).start())

    weight = (w_hi[...], w_lo[...])
    p, z, bias = p_ref[...], z_ref[...], b_ref[...]
    residual = dot3(split(p), weight) + bias - z
    back = dot3(split(residual), weight, NT)

    @pl.when(jnp.logical_not(has_below))
    def _():
        coupling[...] = permuted(order_ref[...], ub_ref[...] - qb_ref[...])

    pl.when(has_below)(lambda: up.wait_recv())
    p = p - step_input * (back + (coupling[...] + p))
    p_all[me] = p
    p_out[...] = p
    pl.when(has_right)(lambda: p_copy(me, True).start())
    pl.when(has_left)(lambda: p_copy(me, False).start())
    pl.when(has_below)(lambda: down.start())

    @pl.when(jnp.logical_not(has_above))
    def _():
        p_next[...] = permuted(order_ref[...], pb_ref[...])

    pt_hi[pl.ds(width, 16), :] = jnp.ones((16, total), jnp.bfloat16)
    pt_lo[pl.ds(width, 16), :] = jnp.zeros((16, total), jnp.bfloat16)

    def block(owner):
        return pl.ds(pl.multiple_of(owner * rows, rows), rows)

    def take_p(owner, value, z_value=None):
        high, low = split(value)
        p_hi[block(owner), :], p_lo[block(owner), :] = high, low
        across = split(value.T)
        pt_hi[pl.ds(0, width), block(owner)] = across[0]
        pt_lo[pl.ds(0, width), block(owner)] = across[1]
        product = dot3((high, low), (w_hi[...], w_lo[...])) + b_ref[...]
        target0[block(owner), :] = product if z_value is None else product - z_value

    take_p(me, p, z)
    for s in range(1, n):
        @pl.when(me >= s)
        def _():
            p_copy(me - s, True).wait_recv()
            pl.when(has_right)(lambda: p_copy(me - s, True).start())
        @pl.when(me + s < n)
        def _():
            p_copy(me + s, False).wait_recv()
            pl.when(has_left)(lambda: p_copy(me + s, False).start())
        if s == n - 1:
            pass
        @pl.when(me >= s)
        def _():
            take_p(me - s, p_all[me - s])
        @pl.when(me + s < n)
        def _():
            take_p(me + s, p_all[me + s])

    def z_arrives(s, use):
        @pl.when(me >= s)
        def _():
            z_copy(me - s, True).wait_recv()
            pl.when(has_right)(lambda: z_copy(me - s, True).start())
        @pl.when(me + s < n)
        def _():
            z_copy(me + s, False).wait_recv()
            pl.when(has_left)(lambda: z_copy(me + s, False).start())
        pl.when(me >= s)(lambda: use(me - s))
        pl.when(me + s < n)(lambda: use(me + s))

    def subtract(owner):
        target0[block(owner), :] -= z_all[owner]

    z_arrives(1, subtract)

    stacked = (p_hi[...], p_lo[...])
    moment = scale * (dot3(stacked, stacked, NT) + 1.0)
    moment_parts = split(moment)
    same = lax.broadcasted_iota(jnp.int32, (total, total), 0) == lax.broadcasted_iota(jnp.int32, (total, total), 1)
    steps = jnp.where(same, 3.0, 0.0) - 3.0 * moment + dot3(moment_parts, moment_parts)
    t = scale * dot3((pt_hi[...], pt_lo[...]), split(steps))
    t_hi[...], t_lo[...] = split(t)
    change[...] = dot3((t_hi[...], t_lo[...]), split(target0[...]))

    def add(owner):
        change[...] -= dot3((t_hi[:, block(owner)], t_lo[:, block(owner)]), split(z_all[owner]))

    for s in range(2, n):
        z_arrives(s, add)

    w = w_ref[...] - change[pl.ds(0, width), :]
    bias = b_ref[...] - change[pl.ds(width, 1), :]
    w_out[...] = w
    b_out[...] = bias
    target = dot3(split(p_all[me]), split(w)) + bias
    z, q, u = z_ref[...], q_ref[...], u_ref[...]
    z = z - step_preact * ((z - target) + (softplus(z) - q) * jax.nn.sigmoid(z))
    z_out[...] = z
    pl.when(has_above)(lambda: down.wait_recv())
    after = p_next[...]
    q = (penalty_nu * softplus(z) + u + penalty_rho * after) / (penalty_nu + penalty_rho)
    q_out[...] = q
    u_out[...] = u + penalty_rho * (after - q)

    for owner in range(n):
        @pl.when(jnp.logical_and(me >= owner, has_right))
        def _():
            z_copy(owner, True).wait_send()
            p_copy(owner, True).wait_send()
        @pl.when(jnp.logical_and(me <= owner, has_left))
        def _():
            z_copy(owner, False).wait_send()
            p_copy(owner, False).wait_send()
    pl.when(has_above)(lambda: up.wait_send())
    pl.when(has_below)(lambda: down.wait_send())


def gathered_body(n, layers, layer_inputs, pre_acts, layer_outputs, multipliers, weights, biases, prev_outputs, prev_multipliers, next_inputs, row_order):
    rows, width = prev_outputs.shape
    total = rows * n
    f32, b16 = jnp.float32, jnp.bfloat16
    dma = pltpu.SemaphoreType.DMA
    vmem = pl.BlockSpec(memory_space=pltpu.VMEM)
    block = jax.ShapeDtypeStruct((rows, width), f32)
    outs = pl.pallas_call(
        functools.partial(kernel, n, layers),
        out_shape=(block,) * 4 + (jax.ShapeDtypeStruct((width, width), f32), jax.ShapeDtypeStruct((1, width), f32)),
        in_specs=[vmem] * 10,
        out_specs=(vmem,) * 6,
        scratch_shapes=[
            pltpu.VMEM((n, rows, width), f32), pltpu.VMEM((n, rows, width), f32),
            pltpu.VMEM((rows, width), f32), pltpu.VMEM((rows, width), f32), pltpu.VMEM((rows, width), f32),
            pltpu.VMEM((width, width), b16), pltpu.VMEM((width, width), b16),
            pltpu.VMEM((total, width), b16), pltpu.VMEM((total, width), b16),
            pltpu.VMEM((width + 16, total), b16), pltpu.VMEM((width + 16, total), b16),
            pltpu.VMEM((total, width), f32),
            pltpu.VMEM((width + 16, total), b16), pltpu.VMEM((width + 16, total), b16),
            pltpu.VMEM((width + 16, width), f32),
            dma((n,)), dma((n,)), dma((n,)), dma((n,)), dma((n,)), dma((n,)), dma((2,)), dma((2,)),
        ],
        compiler_params=pltpu.CompilerParams(collective_id=0, has_side_effects=True, vmem_limit_bytes=48 * 2**20),
    )(layer_inputs[0], pre_acts[0], layer_outputs[0], multipliers[0], weights[0], biases, prev_outputs, prev_multipliers, next_inputs, row_order)
    return tuple(x[None] for x in outs[:5]) + (outs[5],)


def solution(mesh):
    n, layers = mesh.shape["dp"], mesh.shape["layer"]
    body = functools.partial(gathered_body, n, layers) if n <= 8 else summed_body
    return jax.shard_map(
        body,
        mesh=mesh,
        in_specs=(
            P("layer", ("groups", "dp"), None),
            P("layer", ("groups", "dp"), None),
            P("layer", ("groups", "dp"), None),
            P("layer", ("groups", "dp"), None),
            P(("groups", "layer"), None, None),
            P(("groups", "layer"), None),
            P(("groups", "dp"), None),
            P(("groups", "dp"), None),
            P(("groups", "dp"), None),
            P(("groups", "dp"), None),
        ),
        out_specs=(
            P("layer", ("groups", "dp"), None),
            P("layer", ("groups", "dp"), None),
            P("layer", ("groups", "dp"), None),
            P("layer", ("groups", "dp"), None),
            P(("groups", "layer"), None, None),
            P(("groups", "layer"), None),
        ),
        check_vma=False,
    )
```

```python
import functools

import jax
import jax.numpy as jnp
from jax import lax
from jax.experimental import pallas as pl
from jax.experimental.pallas import tpu as pltpu
from jax.sharding import PartitionSpec as P

INNER = 3


penalty_nu = 1.0
penalty_rho = 1.0
step_input = 0.2
step_weight = 0.3
step_preact = 0.5


def from_behind(x, axis, by):
    count = lax.axis_size(axis)
    pairs = [(i, i + by) for i in range(count) if 0 <= i + by < count]
    return lax.ppermute(x, axis, pairs)


def matmul(left, right):
    return jnp.dot(left, right, precision=lax.Precision.HIGHEST)


def summed_body(
    layer_inputs,
    pre_acts,
    layer_outputs,
    multipliers,
    weights,
    biases,
    prev_outputs,
    prev_multipliers,
    next_inputs,
    row_order,
):
    row_perm = row_order[0]
    edge_outputs = jnp.take(prev_outputs, row_perm, axis=0)
    edge_duals = jnp.take(prev_multipliers, row_perm, axis=0)
    edge_inputs = jnp.take(next_inputs, row_perm, axis=0)
    first_layer = lax.axis_index("layer") == 0
    last_layer = lax.axis_index("layer") == lax.axis_size("layer") - 1
    row_count = layer_inputs.shape[1] * lax.axis_size("dp")
    scale = step_weight / row_count
    inputs, preact, outputs, duals = (
        layer_inputs[0],
        pre_acts[0],
        layer_outputs[0],
        multipliers[0],
    )
    weight, offset = (weights[0], biases[0])
    before_out, before_dual = from_behind((outputs, duals), "layer", 1)
    before_out = jnp.where(first_layer, edge_outputs, before_out)
    before_dual = jnp.where(first_layer, edge_duals, before_dual)
    coupling = before_dual + penalty_rho * (inputs - before_out)
    residual = matmul(inputs, weight) + offset[None, :] - preact
    inputs = inputs - step_input * (penalty_nu * matmul(residual, weight.T) + coupling)
    gram_matrix, cross_term, column_sums, preact_sums = lax.psum(
        (
            matmul(inputs.T, inputs),
            matmul(inputs.T, preact),
            jnp.sum(inputs, axis=0),
            jnp.sum(preact, axis=0),
        ),
        "dp",
    )
    for inner_step in range(INNER):
        grad_weight = (
            matmul(gram_matrix, weight) + column_sums[:, None] * offset[None, :] - cross_term
        )
        grad_offset = matmul(column_sums[None, :], weight)[0] + row_count * offset - preact_sums
        weight = weight - scale * grad_weight
        offset = offset - scale * grad_offset
    target = matmul(inputs, weight) + offset[None, :]
    preact = preact - step_preact * (
        preact - target + (jax.nn.softplus(preact) - outputs) * jax.nn.sigmoid(preact)
    )
    after_in = from_behind(inputs, "layer", -1)
    after_in = jnp.where(last_layer, edge_inputs, after_in)
    outputs = (penalty_nu * jax.nn.softplus(preact) + duals + penalty_rho * after_in) / (
        penalty_nu + penalty_rho
    )
    duals = duals + penalty_rho * (after_in - outputs)
    return (inputs[None], preact[None], outputs[None], duals[None], weight[None], offset[None])


MESH = pl.DeviceIdType.MESH
NN = (((1,), (0,)), ((), ()))
NT = (((1,), (1,)), ((), ()))


def split(x):
    high = x.astype(jnp.bfloat16)
    return high, (x - high.astype(jnp.float32)).astype(jnp.bfloat16)


def dot3(left, right, dims=NN):
    def one(a, b):
        return lax.dot_general(a, b, dims, preferred_element_type=jnp.float32)

    return one(left[0], right[0]) + (one(left[0], right[1]) + one(left[1], right[0]))


def softplus(v):
    return jnp.maximum(v, 0.0) + jnp.log1p(jnp.exp(-jnp.abs(v)))


def permuted(order, x):
    rows = x.shape[0]
    stored = lax.broadcasted_iota(jnp.int32, (rows, rows), 0)
    pick = jnp.where(stored == order, 1.0, 0.0).T.astype(jnp.bfloat16)
    high, rest = split(x)
    rest = x - high.astype(jnp.float32)
    mid, low = split(rest)

    def one(part):
        return jnp.dot(pick, part, preferred_element_type=jnp.float32)

    return one(high) + (one(mid) + one(low))


def kernel(
    n, layers,
    p_hbm, z_hbm, q_hbm, u_hbm, w_hbm, b_hbm, qb_hbm, ub_hbm, pb_hbm, order_hbm,
    p_out, z_out, q_out, u_out, w_out, b_out,
    p_ref, z_ref, q_ref, u_ref, w_ref, b_ref, qb_ref, ub_ref, pb_ref, order_ref,
    p_all, z_all, coupling, p_next, own_coupling, w_hi, w_lo, p_hi, p_lo, pt_hi, pt_lo, target0, t_hi, t_lo, change,
    z_right, z_left, z_recv, p_right, p_left, p_recv, layer_send, layer_recv, loads, stores, z_new,
):
    rows, width = p_ref.shape
    total = rows * n
    me, layer = lax.axis_index("dp"), lax.axis_index("layer")
    scale = step_weight / total
    has_left, has_right = me > 0, me < n - 1
    has_below, has_above = layer > 0, layer < layers - 1

    barrier = pltpu.get_barrier_semaphore()
    for there, axis, index in (
        (has_left, "dp", me - 1), (has_right, "dp", me + 1),
        (has_below, "layer", layer - 1), (has_above, "layer", layer + 1),
    ):
        @pl.when(there)
        def _():
            pl.semaphore_signal(barrier, inc=1, device_id={axis: index}, device_id_type=MESH)

    load = {}
    for i, (name, source, target) in enumerate((
        ("u", u_hbm, u_ref), ("q", q_hbm, q_ref), ("z", z_hbm, z_ref), ("w", w_hbm, w_ref), ("p", p_hbm, p_ref),
        ("b", b_hbm, b_ref), ("order", order_hbm, order_ref), ("ub", ub_hbm, ub_ref), ("qb", qb_hbm, qb_ref),
        ("pb", pb_hbm, pb_ref),
    )):
        load[name] = pltpu.make_async_copy(source, target, loads.at[i])
        load[name].start()
    load["u"].wait()
    load["q"].wait()
    own_coupling[...] = u_ref[...] - q_ref[...]
    load["z"].wait()
    ends = [jnp.where(there, 1, 0) for there in (has_left, has_right, has_below, has_above)]
    pl.semaphore_wait(barrier, ends[0] + ends[1] + ends[2] + ends[3])

    def z_copy(owner, to_right, own=False):
        return pltpu.make_async_remote_copy(
            src_ref=z_ref if own else z_all.at[owner], dst_ref=z_all.at[owner],
            send_sem=(z_right if to_right else z_left).at[owner], recv_sem=z_recv.at[owner],
            device_id={"dp": me + 1 if to_right else me - 1}, device_id_type=MESH,
        )

    def p_copy(owner, to_right):
        return pltpu.make_async_remote_copy(
            src_ref=p_all.at[owner], dst_ref=p_all.at[owner],
            send_sem=(p_right if to_right else p_left).at[owner], recv_sem=p_recv.at[owner],
            device_id={"dp": me + 1 if to_right else me - 1}, device_id_type=MESH,
        )

    up = pltpu.make_async_remote_copy(
        src_ref=own_coupling, dst_ref=coupling, send_sem=layer_send.at[0], recv_sem=layer_recv.at[0],
        device_id={"layer": layer + 1}, device_id_type=MESH,
    )
    down = pltpu.make_async_remote_copy(
        src_ref=p_all.at[me], dst_ref=p_next, send_sem=layer_send.at[1], recv_sem=layer_recv.at[1],
        device_id={"layer": layer - 1}, device_id_type=MESH,
    )

    pl.when(has_above)(lambda: up.start())
    pl.when(has_right)(lambda: z_copy(me, True, True).start())
    pl.when(has_left)(lambda: z_copy(me, False, True).start())

    for name in ("w", "p", "b", "order", "ub", "qb", "pb"):
        load[name].wait()
    w_hi[...], w_lo[...] = split(w_ref[...])
    weight = (w_hi[...], w_lo[...])
    p, z, bias = p_ref[...], z_ref[...], b_ref[...]
    residual = dot3(split(p), weight) + bias - z
    back = dot3(split(residual), weight, NT)

    @pl.when(jnp.logical_not(has_below))
    def _():
        coupling[...] = permuted(order_ref[...], ub_ref[...] - qb_ref[...])

    pl.when(has_below)(lambda: up.wait_recv())
    p = p - step_input * (back + (coupling[...] + p))
    p_all[me] = p
    store = {}
    for i, (name, source, target) in enumerate((
        ("p", p_all.at[me], p_out), ("w", w_ref, w_out), ("b", b_ref, b_out), ("z", z_new, z_out), ("q", q_ref, q_out), ("u", u_ref, u_out),
    )):
        store[name] = pltpu.make_async_copy(source, target, stores.at[i])
    store["p"].start()
    pl.when(has_right)(lambda: p_copy(me, True).start())
    pl.when(has_left)(lambda: p_copy(me, False).start())
    pl.when(has_below)(lambda: down.start())

    @pl.when(jnp.logical_not(has_above))
    def _():
        p_next[...] = permuted(order_ref[...], pb_ref[...])

    pt_hi[pl.ds(width, 16), :] = jnp.ones((16, total), jnp.bfloat16)
    pt_lo[pl.ds(width, 16), :] = jnp.zeros((16, total), jnp.bfloat16)

    def block(owner):
        return pl.ds(pl.multiple_of(owner * rows, rows), rows)

    def take_p(owner, value, z_value=None):
        high, low = split(value)
        p_hi[block(owner), :], p_lo[block(owner), :] = high, low
        across = split(value.T)
        pt_hi[pl.ds(0, width), block(owner)] = across[0]
        pt_lo[pl.ds(0, width), block(owner)] = across[1]
        product = dot3((high, low), (w_hi[...], w_lo[...])) + b_ref[...]
        target0[block(owner), :] = product if z_value is None else product - z_value

    take_p(me, p, z)
    for s in range(1, n):
        @pl.when(me >= s)
        def _():
            p_copy(me - s, True).wait_recv()
            pl.when(has_right)(lambda: p_copy(me - s, True).start())
        @pl.when(me + s < n)
        def _():
            p_copy(me + s, False).wait_recv()
            pl.when(has_left)(lambda: p_copy(me + s, False).start())
        if s == n - 1:
            pass
        @pl.when(me >= s)
        def _():
            take_p(me - s, p_all[me - s])
        @pl.when(me + s < n)
        def _():
            take_p(me + s, p_all[me + s])

    def z_arrives(s, use):
        @pl.when(me >= s)
        def _():
            z_copy(me - s, True).wait_recv()
            pl.when(has_right)(lambda: z_copy(me - s, True).start())
        @pl.when(me + s < n)
        def _():
            z_copy(me + s, False).wait_recv()
            pl.when(has_left)(lambda: z_copy(me + s, False).start())
        pl.when(me >= s)(lambda: use(me - s))
        pl.when(me + s < n)(lambda: use(me + s))

    def subtract(owner):
        target0[block(owner), :] -= z_all[owner]

    z_arrives(1, subtract)

    stacked = (p_hi[...], p_lo[...])
    moment = scale * (dot3(stacked, stacked, NT) + 1.0)
    moment_parts = split(moment)
    same = lax.broadcasted_iota(jnp.int32, (total, total), 0) == lax.broadcasted_iota(jnp.int32, (total, total), 1)
    steps = jnp.where(same, 3.0, 0.0) - 3.0 * moment + dot3(moment_parts, moment_parts)
    t = scale * dot3((pt_hi[...], pt_lo[...]), split(steps))
    t_hi[...], t_lo[...] = split(t)
    change[...] = dot3((t_hi[...], t_lo[...]), split(target0[...]))

    def add(owner):
        change[...] -= dot3((t_hi[:, block(owner)], t_lo[:, block(owner)]), split(z_all[owner]))

    for s in range(2, n):
        z_arrives(s, add)

    w = w_ref[...] - change[pl.ds(0, width), :]
    bias = b_ref[...] - change[pl.ds(width, 1), :]
    w_ref[...] = w
    b_ref[...] = bias
    store["w"].start()
    store["b"].start()
    target = dot3(split(p_all[me]), split(w)) + bias
    z, q, u = z_ref[...], q_ref[...], u_ref[...]
    z = z - step_preact * ((z - target) + (softplus(z) - q) * jax.nn.sigmoid(z))
    z_new[...] = z
    store["z"].start()
    pl.when(has_above)(lambda: down.wait_recv())
    after = p_next[...]
    q = (penalty_nu * softplus(z) + u + penalty_rho * after) / (penalty_nu + penalty_rho)
    q_ref[...] = q
    store["q"].start()
    u_ref[...] = u + penalty_rho * (after - q)
    store["u"].start()

    for owner in range(n):
        @pl.when(jnp.logical_and(me >= owner, has_right))
        def _():
            z_copy(owner, True).wait_send()
            p_copy(owner, True).wait_send()
        @pl.when(jnp.logical_and(me <= owner, has_left))
        def _():
            z_copy(owner, False).wait_send()
            p_copy(owner, False).wait_send()
    pl.when(has_above)(lambda: up.wait_send())
    pl.when(has_below)(lambda: down.wait_send())
    for copy in store.values():
        copy.wait()


def store_kernel(*refs):
    sources, targets, held, sems = refs[:6], refs[6:12], refs[12:18], refs[18]
    ins = [pltpu.make_async_copy(a, b, sems.at[0, i]) for i, (a, b) in enumerate(zip(sources, held))]
    outs = [pltpu.make_async_copy(a, b, sems.at[1, i]) for i, (a, b) in enumerate(zip(held, targets))]
    for copy in ins:
        copy.start()
    for taken, copy in zip(ins, outs):
        taken.wait()
        copy.start()
    for copy in outs:
        copy.wait()


def gathered_body(n, layers, layer_inputs, pre_acts, layer_outputs, multipliers, weights, biases, prev_outputs, prev_multipliers, next_inputs, row_order):
    rows, width = prev_outputs.shape
    total = rows * n
    f32, b16 = jnp.float32, jnp.bfloat16
    dma = pltpu.SemaphoreType.DMA
    block = jax.ShapeDtypeStruct((rows, width), f32)
    hbm = pl.BlockSpec(memory_space=pltpu.HBM)
    shapes = (block,) * 4 + (jax.ShapeDtypeStruct((width, width), f32), jax.ShapeDtypeStruct((1, width), f32))
    outs = pl.pallas_call(
        functools.partial(kernel, n, layers),
        out_shape=shapes,
        in_specs=[hbm] * 10,
        out_specs=(hbm,) * 6,
        scratch_shapes=[
            *(pltpu.VMEM((rows, width), f32),) * 4,
            pltpu.VMEM((width, width), f32), pltpu.VMEM((1, width), f32),
            *(pltpu.VMEM((rows, width), f32),) * 3,
            pltpu.VMEM((1, rows), jnp.int32),
            pltpu.VMEM((n, rows, width), f32), pltpu.VMEM((n, rows, width), f32),
            pltpu.VMEM((rows, width), f32), pltpu.VMEM((rows, width), f32), pltpu.VMEM((rows, width), f32),
            pltpu.VMEM((width, width), b16), pltpu.VMEM((width, width), b16),
            pltpu.VMEM((total, width), b16), pltpu.VMEM((total, width), b16),
            pltpu.VMEM((width + 16, total), b16), pltpu.VMEM((width + 16, total), b16),
            pltpu.VMEM((total, width), f32),
            pltpu.VMEM((width + 16, total), b16), pltpu.VMEM((width + 16, total), b16),
            pltpu.VMEM((width + 16, width), f32),
            dma((n,)), dma((n,)), dma((n,)), dma((n,)), dma((n,)), dma((n,)), dma((2,)), dma((2,)), dma((10,)), dma((6,)), pltpu.VMEM((rows, width), f32),
        ],
        compiler_params=pltpu.CompilerParams(collective_id=0, has_side_effects=True),
    )(layer_inputs[0], pre_acts[0], layer_outputs[0], multipliers[0], weights[0], biases, prev_outputs, prev_multipliers, next_inputs, row_order)
    outs = pl.pallas_call(
        store_kernel, out_shape=shapes, in_specs=[hbm] * 6, out_specs=(hbm,) * 6,
        scratch_shapes=[*(pltpu.VMEM(x.shape, x.dtype) for x in shapes), dma((2, 6))],
    )(*outs)
    return tuple(x[None] for x in outs[:5]) + (outs[5],)


def solution(mesh):
    n, layers = mesh.shape["dp"], mesh.shape["layer"]
    body = functools.partial(gathered_body, n, layers) if n <= 8 else summed_body
    return jax.shard_map(
        body,
        mesh=mesh,
        in_specs=(
            P("layer", ("groups", "dp"), None),
            P("layer", ("groups", "dp"), None),
            P("layer", ("groups", "dp"), None),
            P("layer", ("groups", "dp"), None),
            P(("groups", "layer"), None, None),
            P(("groups", "layer"), None),
            P(("groups", "dp"), None),
            P(("groups", "dp"), None),
            P(("groups", "dp"), None),
            P(("groups", "dp"), None),
        ),
        out_specs=(
            P("layer", ("groups", "dp"), None),
            P("layer", ("groups", "dp"), None),
            P("layer", ("groups", "dp"), None),
            P("layer", ("groups", "dp"), None),
            P(("groups", "layer"), None, None),
            P(("groups", "layer"), None),
        ),
        check_vma=False,
    )
```

```python
import functools

import jax
import jax.numpy as jnp
from jax import lax
from jax.experimental import pallas as pl
from jax.experimental.pallas import tpu as pltpu
from jax.sharding import PartitionSpec as P

INNER = 3


penalty_nu = 1.0
penalty_rho = 1.0
step_input = 0.2
step_weight = 0.3
step_preact = 0.5


def from_behind(x, axis, by):
    count = lax.axis_size(axis)
    pairs = [(i, i + by) for i in range(count) if 0 <= i + by < count]
    return lax.ppermute(x, axis, pairs)


def matmul(left, right):
    return jnp.dot(left, right, precision=lax.Precision.HIGHEST)


def summed_body(
    layer_inputs,
    pre_acts,
    layer_outputs,
    multipliers,
    weights,
    biases,
    prev_outputs,
    prev_multipliers,
    next_inputs,
    row_order,
):
    row_perm = row_order[0]
    edge_outputs = jnp.take(prev_outputs, row_perm, axis=0)
    edge_duals = jnp.take(prev_multipliers, row_perm, axis=0)
    edge_inputs = jnp.take(next_inputs, row_perm, axis=0)
    first_layer = lax.axis_index("layer") == 0
    last_layer = lax.axis_index("layer") == lax.axis_size("layer") - 1
    row_count = layer_inputs.shape[1] * lax.axis_size("dp")
    scale = step_weight / row_count
    inputs, preact, outputs, duals = (
        layer_inputs[0],
        pre_acts[0],
        layer_outputs[0],
        multipliers[0],
    )
    weight, offset = (weights[0], biases[0])
    before_out, before_dual = from_behind((outputs, duals), "layer", 1)
    before_out = jnp.where(first_layer, edge_outputs, before_out)
    before_dual = jnp.where(first_layer, edge_duals, before_dual)
    coupling = before_dual + penalty_rho * (inputs - before_out)
    residual = matmul(inputs, weight) + offset[None, :] - preact
    inputs = inputs - step_input * (penalty_nu * matmul(residual, weight.T) + coupling)
    gram_matrix, cross_term, column_sums, preact_sums = lax.psum(
        (
            matmul(inputs.T, inputs),
            matmul(inputs.T, preact),
            jnp.sum(inputs, axis=0),
            jnp.sum(preact, axis=0),
        ),
        "dp",
    )
    for inner_step in range(INNER):
        grad_weight = (
            matmul(gram_matrix, weight) + column_sums[:, None] * offset[None, :] - cross_term
        )
        grad_offset = matmul(column_sums[None, :], weight)[0] + row_count * offset - preact_sums
        weight = weight - scale * grad_weight
        offset = offset - scale * grad_offset
    target = matmul(inputs, weight) + offset[None, :]
    preact = preact - step_preact * (
        preact - target + (jax.nn.softplus(preact) - outputs) * jax.nn.sigmoid(preact)
    )
    after_in = from_behind(inputs, "layer", -1)
    after_in = jnp.where(last_layer, edge_inputs, after_in)
    outputs = (penalty_nu * jax.nn.softplus(preact) + duals + penalty_rho * after_in) / (
        penalty_nu + penalty_rho
    )
    duals = duals + penalty_rho * (after_in - outputs)
    return (inputs[None], preact[None], outputs[None], duals[None], weight[None], offset[None])


MESH = pl.DeviceIdType.MESH
NN = (((1,), (0,)), ((), ()))
NT = (((1,), (1,)), ((), ()))


def split(x):
    high = x.astype(jnp.bfloat16)
    return high, (x - high.astype(jnp.float32)).astype(jnp.bfloat16)


def dot3(left, right, dims=NN):
    def one(a, b):
        return lax.dot_general(a, b, dims, preferred_element_type=jnp.float32)

    return one(left[0], right[0]) + (one(left[0], right[1]) + one(left[1], right[0]))


def softplus(v):
    return jnp.maximum(v, 0.0) + jnp.log1p(jnp.exp(-jnp.abs(v)))


def permuted(order, x):
    rows = x.shape[0]
    stored = lax.broadcasted_iota(jnp.int32, (rows, rows), 0)
    pick = jnp.where(stored == order, 1.0, 0.0).T.astype(jnp.bfloat16)
    high, rest = split(x)
    rest = x - high.astype(jnp.float32)
    mid, low = split(rest)

    def one(part):
        return jnp.dot(pick, part, preferred_element_type=jnp.float32)

    return one(high) + (one(mid) + one(low))


def kernel(
    n, layers,
    p_hbm, z_hbm, q_hbm, u_hbm, w_hbm, b_hbm, qb_hbm, ub_hbm, pb_hbm, order_hbm,
    p_out, z_out, q_out, u_out, w_out, b_out,
    p_ref, z_ref, q_ref, u_ref, w_ref, b_ref, qb_ref, ub_ref, pb_ref, order_ref,
    p_all, z_all, coupling, p_next, own_coupling, w_hi, w_lo, p_hi, p_lo, pt_hi, pt_lo, target0, t_hi, t_lo, change,
    z_right, z_left, z_recv, p_right, p_left, p_recv, layer_send, layer_recv, loads, stores, z_new,
):
    rows, width = p_ref.shape
    total = rows * n
    me, layer = lax.axis_index("dp"), lax.axis_index("layer")
    scale = step_weight / total
    has_left, has_right = me > 0, me < n - 1
    has_below, has_above = layer > 0, layer < layers - 1

    barrier = pltpu.get_barrier_semaphore()
    for there, axis, index in (
        (has_left, "dp", me - 1), (has_right, "dp", me + 1),
        (has_below, "layer", layer - 1), (has_above, "layer", layer + 1),
    ):
        @pl.when(there)
        def _():
            pl.semaphore_signal(barrier, inc=1, device_id={axis: index}, device_id_type=MESH)

    load = {}
    for i, (name, source, target) in enumerate((
        ("z", z_hbm, z_ref), ("u", u_hbm, u_ref), ("q", q_hbm, q_ref), ("w", w_hbm, w_ref), ("p", p_hbm, p_ref),
        ("b", b_hbm, b_ref), ("order", order_hbm, order_ref), ("ub", ub_hbm, ub_ref), ("qb", qb_hbm, qb_ref),
        ("pb", pb_hbm, pb_ref),
    )):
        load[name] = pltpu.make_async_copy(source, target, loads.at[i])
        load[name].start()
    load["z"].wait()
    ends = [jnp.where(there, 1, 0) for there in (has_left, has_right, has_below, has_above)]
    pl.semaphore_wait(barrier, ends[0] + ends[1] + ends[2] + ends[3])

    def z_copy(owner, to_right, own=False):
        return pltpu.make_async_remote_copy(
            src_ref=z_ref if own else z_all.at[owner], dst_ref=z_all.at[owner],
            send_sem=(z_right if to_right else z_left).at[owner], recv_sem=z_recv.at[owner],
            device_id={"dp": me + 1 if to_right else me - 1}, device_id_type=MESH,
        )

    def p_copy(owner, to_right):
        return pltpu.make_async_remote_copy(
            src_ref=p_all.at[owner], dst_ref=p_all.at[owner],
            send_sem=(p_right if to_right else p_left).at[owner], recv_sem=p_recv.at[owner],
            device_id={"dp": me + 1 if to_right else me - 1}, device_id_type=MESH,
        )

    up = pltpu.make_async_remote_copy(
        src_ref=own_coupling, dst_ref=coupling, send_sem=layer_send.at[0], recv_sem=layer_recv.at[0],
        device_id={"layer": layer + 1}, device_id_type=MESH,
    )
    down = pltpu.make_async_remote_copy(
        src_ref=p_all.at[me], dst_ref=p_next, send_sem=layer_send.at[1], recv_sem=layer_recv.at[1],
        device_id={"layer": layer - 1}, device_id_type=MESH,
    )

    pl.when(has_right)(lambda: z_copy(me, True, True).start())
    pl.when(has_left)(lambda: z_copy(me, False, True).start())
    load["u"].wait()
    load["q"].wait()
    own_coupling[...] = u_ref[...] - q_ref[...]
    pl.when(has_above)(lambda: up.start())

    for name in ("w", "p", "b", "order", "ub", "qb", "pb"):
        load[name].wait()
    w_hi[...], w_lo[...] = split(w_ref[...])
    weight = (w_hi[...], w_lo[...])
    p, z, bias = p_ref[...], z_ref[...], b_ref[...]
    residual = dot3(split(p), weight) + bias - z
    back = dot3(split(residual), weight, NT)

    @pl.when(jnp.logical_not(has_below))
    def _():
        coupling[...] = permuted(order_ref[...], ub_ref[...] - qb_ref[...])

    pl.when(has_below)(lambda: up.wait_recv())
    p = p - step_input * (back + (coupling[...] + p))
    p_all[me] = p
    store = {}
    for i, (name, source, target) in enumerate((
        ("p", p_all.at[me], p_out), ("w", w_ref, w_out), ("b", b_ref, b_out), ("z", z_new, z_out), ("q", q_ref, q_out), ("u", u_ref, u_out),
    )):
        store[name] = pltpu.make_async_copy(source, target, stores.at[i])
    store["p"].start()
    pl.when(has_right)(lambda: p_copy(me, True).start())
    pl.when(has_left)(lambda: p_copy(me, False).start())
    pl.when(has_below)(lambda: down.start())

    @pl.when(jnp.logical_not(has_above))
    def _():
        p_next[...] = permuted(order_ref[...], pb_ref[...])

    pt_hi[pl.ds(width, 16), :] = jnp.ones((16, total), jnp.bfloat16)
    pt_lo[pl.ds(width, 16), :] = jnp.zeros((16, total), jnp.bfloat16)

    def block(owner):
        return pl.ds(pl.multiple_of(owner * rows, rows), rows)

    def take_p(owner, value, z_value=None):
        high, low = split(value)
        p_hi[block(owner), :], p_lo[block(owner), :] = high, low
        across = split(value.T)
        pt_hi[pl.ds(0, width), block(owner)] = across[0]
        pt_lo[pl.ds(0, width), block(owner)] = across[1]
        product = dot3((high, low), (w_hi[...], w_lo[...])) + b_ref[...]
        target0[block(owner), :] = product if z_value is None else product - z_value

    def relay(s, copy):
        @pl.when(me >= s)
        def _():
            copy(me - s, True).wait_recv()
            pl.when(has_right)(lambda: copy(me - s, True).start())

        @pl.when(me + s < n)
        def _():
            copy(me + s, False).wait_recv()
            pl.when(has_left)(lambda: copy(me + s, False).start())

    def use(s, step):
        pl.when(me >= s)(lambda: step(me - s))
        pl.when(me + s < n)(lambda: step(me + s))

    take_p(me, p, z)
    for s in range(1, n):
        relay(s, p_copy)
        if s < n - 1:
            relay(s, z_copy)
        use(s, lambda owner: take_p(owner, p_all[owner], z_all[owner] if s < n - 1 else None))

    stacked = (p_hi[...], p_lo[...])
    moment = scale * (dot3(stacked, stacked, NT) + 1.0)
    moment_parts = split(moment)
    same = lax.broadcasted_iota(jnp.int32, (total, total), 0) == lax.broadcasted_iota(jnp.int32, (total, total), 1)
    steps = jnp.where(same, 3.0, 0.0) - 3.0 * moment + dot3(moment_parts, moment_parts)
    t = scale * dot3((pt_hi[...], pt_lo[...]), split(steps))
    t_hi[...], t_lo[...] = split(t)
    change[...] = dot3((t_hi[...], t_lo[...]), split(target0[...]))

    def add(owner):
        change[...] -= dot3((t_hi[:, block(owner)], t_lo[:, block(owner)]), split(z_all[owner]))

    if n > 1:
        relay(n - 1, z_copy)
        use(n - 1, add)

    w = w_ref[...] - change[pl.ds(0, width), :]
    bias = b_ref[...] - change[pl.ds(width, 1), :]
    w_ref[...] = w
    b_ref[...] = bias
    store["w"].start()
    store["b"].start()
    target = dot3(split(p_all[me]), split(w)) + bias
    z, q, u = z_ref[...], q_ref[...], u_ref[...]
    z = z - step_preact * ((z - target) + (softplus(z) - q) * jax.nn.sigmoid(z))
    z_new[...] = z
    store["z"].start()
    pl.when(has_above)(lambda: down.wait_recv())
    after = p_next[...]
    q = (penalty_nu * softplus(z) + u + penalty_rho * after) / (penalty_nu + penalty_rho)
    q_ref[...] = q
    store["q"].start()
    u_ref[...] = u + penalty_rho * (after - q)
    store["u"].start()

    for owner in range(n):
        @pl.when(jnp.logical_and(me >= owner, has_right))
        def _():
            z_copy(owner, True).wait_send()
            p_copy(owner, True).wait_send()
        @pl.when(jnp.logical_and(me <= owner, has_left))
        def _():
            z_copy(owner, False).wait_send()
            p_copy(owner, False).wait_send()
    pl.when(has_above)(lambda: up.wait_send())
    pl.when(has_below)(lambda: down.wait_send())
    for copy in store.values():
        copy.wait()


def store_kernel(*refs):
    sources, targets, held, sems = refs[:6], refs[6:12], refs[12:18], refs[18]
    ins = [pltpu.make_async_copy(a, b, sems.at[0, i]) for i, (a, b) in enumerate(zip(sources, held))]
    outs = [pltpu.make_async_copy(a, b, sems.at[1, i]) for i, (a, b) in enumerate(zip(held, targets))]
    for copy in ins:
        copy.start()
    for taken, copy in zip(ins, outs):
        taken.wait()
        copy.start()
    for copy in outs:
        copy.wait()


def gathered_body(n, layers, layer_inputs, pre_acts, layer_outputs, multipliers, weights, biases, prev_outputs, prev_multipliers, next_inputs, row_order):
    rows, width = prev_outputs.shape
    total = rows * n
    f32, b16 = jnp.float32, jnp.bfloat16
    dma = pltpu.SemaphoreType.DMA
    block = jax.ShapeDtypeStruct((rows, width), f32)
    hbm = pl.BlockSpec(memory_space=pltpu.HBM)
    shapes = (block,) * 4 + (jax.ShapeDtypeStruct((width, width), f32), jax.ShapeDtypeStruct((1, width), f32))
    outs = pl.pallas_call(
        functools.partial(kernel, n, layers),
        out_shape=shapes,
        in_specs=[hbm] * 10,
        out_specs=(hbm,) * 6,
        scratch_shapes=[
            *(pltpu.VMEM((rows, width), f32),) * 4,
            pltpu.VMEM((width, width), f32), pltpu.VMEM((1, width), f32),
            *(pltpu.VMEM((rows, width), f32),) * 3,
            pltpu.VMEM((1, rows), jnp.int32),
            pltpu.VMEM((n, rows, width), f32), pltpu.VMEM((n, rows, width), f32),
            pltpu.VMEM((rows, width), f32), pltpu.VMEM((rows, width), f32), pltpu.VMEM((rows, width), f32),
            pltpu.VMEM((width, width), b16), pltpu.VMEM((width, width), b16),
            pltpu.VMEM((total, width), b16), pltpu.VMEM((total, width), b16),
            pltpu.VMEM((width + 16, total), b16), pltpu.VMEM((width + 16, total), b16),
            pltpu.VMEM((total, width), f32),
            pltpu.VMEM((width + 16, total), b16), pltpu.VMEM((width + 16, total), b16),
            pltpu.VMEM((width + 16, width), f32),
            dma((n,)), dma((n,)), dma((n,)), dma((n,)), dma((n,)), dma((n,)), dma((2,)), dma((2,)), dma((10,)), dma((6,)), pltpu.VMEM((rows, width), f32),
        ],
        compiler_params=pltpu.CompilerParams(collective_id=0, has_side_effects=True),
    )(layer_inputs[0], pre_acts[0], layer_outputs[0], multipliers[0], weights[0], biases, prev_outputs, prev_multipliers, next_inputs, row_order)
    outs = pl.pallas_call(
        store_kernel, out_shape=shapes, in_specs=[hbm] * 6, out_specs=(hbm,) * 6,
        scratch_shapes=[*(pltpu.VMEM(x.shape, x.dtype) for x in shapes), dma((2, 6))],
    )(*outs)
    return tuple(x[None] for x in outs[:5]) + (outs[5],)


def solution(mesh):
    n, layers = mesh.shape["dp"], mesh.shape["layer"]
    body = functools.partial(gathered_body, n, layers) if n <= 8 else summed_body
    return jax.shard_map(
        body,
        mesh=mesh,
        in_specs=(
            P("layer", ("groups", "dp"), None),
            P("layer", ("groups", "dp"), None),
            P("layer", ("groups", "dp"), None),
            P("layer", ("groups", "dp"), None),
            P(("groups", "layer"), None, None),
            P(("groups", "layer"), None),
            P(("groups", "dp"), None),
            P(("groups", "dp"), None),
            P(("groups", "dp"), None),
            P(("groups", "dp"), None),
        ),
        out_specs=(
            P("layer", ("groups", "dp"), None),
            P("layer", ("groups", "dp"), None),
            P("layer", ("groups", "dp"), None),
            P("layer", ("groups", "dp"), None),
            P(("groups", "layer"), None, None),
            P(("groups", "layer"), None),
        ),
        check_vma=False,
    )
```

```python
import functools

import jax
import jax.numpy as jnp
from jax import lax
from jax.experimental import pallas as pl
from jax.experimental.pallas import tpu as pltpu
from jax.sharding import PartitionSpec as P

INNER = 3


penalty_nu = 1.0
penalty_rho = 1.0
step_input = 0.2
step_weight = 0.3
step_preact = 0.5


def from_behind(x, axis, by):
    count = lax.axis_size(axis)
    pairs = [(i, i + by) for i in range(count) if 0 <= i + by < count]
    return lax.ppermute(x, axis, pairs)


def matmul(left, right):
    return jnp.dot(left, right, precision=lax.Precision.HIGHEST)


def summed_body(
    layer_inputs,
    pre_acts,
    layer_outputs,
    multipliers,
    weights,
    biases,
    prev_outputs,
    prev_multipliers,
    next_inputs,
    row_order,
):
    row_perm = row_order[0]
    edge_outputs = jnp.take(prev_outputs, row_perm, axis=0)
    edge_duals = jnp.take(prev_multipliers, row_perm, axis=0)
    edge_inputs = jnp.take(next_inputs, row_perm, axis=0)
    first_layer = lax.axis_index("layer") == 0
    last_layer = lax.axis_index("layer") == lax.axis_size("layer") - 1
    row_count = layer_inputs.shape[1] * lax.axis_size("dp")
    scale = step_weight / row_count
    inputs, preact, outputs, duals = (
        layer_inputs[0],
        pre_acts[0],
        layer_outputs[0],
        multipliers[0],
    )
    weight, offset = (weights[0], biases[0])
    before_out, before_dual = from_behind((outputs, duals), "layer", 1)
    before_out = jnp.where(first_layer, edge_outputs, before_out)
    before_dual = jnp.where(first_layer, edge_duals, before_dual)
    coupling = before_dual + penalty_rho * (inputs - before_out)
    residual = matmul(inputs, weight) + offset[None, :] - preact
    inputs = inputs - step_input * (penalty_nu * matmul(residual, weight.T) + coupling)
    gram_matrix, cross_term, column_sums, preact_sums = lax.psum(
        (
            matmul(inputs.T, inputs),
            matmul(inputs.T, preact),
            jnp.sum(inputs, axis=0),
            jnp.sum(preact, axis=0),
        ),
        "dp",
    )
    for inner_step in range(INNER):
        grad_weight = (
            matmul(gram_matrix, weight) + column_sums[:, None] * offset[None, :] - cross_term
        )
        grad_offset = matmul(column_sums[None, :], weight)[0] + row_count * offset - preact_sums
        weight = weight - scale * grad_weight
        offset = offset - scale * grad_offset
    target = matmul(inputs, weight) + offset[None, :]
    preact = preact - step_preact * (
        preact - target + (jax.nn.softplus(preact) - outputs) * jax.nn.sigmoid(preact)
    )
    after_in = from_behind(inputs, "layer", -1)
    after_in = jnp.where(last_layer, edge_inputs, after_in)
    outputs = (penalty_nu * jax.nn.softplus(preact) + duals + penalty_rho * after_in) / (
        penalty_nu + penalty_rho
    )
    duals = duals + penalty_rho * (after_in - outputs)
    return (inputs[None], preact[None], outputs[None], duals[None], weight[None], offset[None])


MESH = pl.DeviceIdType.MESH
VMEM_BYTES = 67043328
NN = (((1,), (0,)), ((), ()))
NT = (((1,), (1,)), ((), ()))


def split(x):
    high = x.astype(jnp.bfloat16)
    return high, (x - high.astype(jnp.float32)).astype(jnp.bfloat16)


def dot3(left, right, dims=NN):
    def one(a, b):
        return lax.dot_general(a, b, dims, preferred_element_type=jnp.float32)

    return one(left[0], right[0]) + (one(left[0], right[1]) + one(left[1], right[0]))


def softplus(v):
    return jnp.maximum(v, 0.0) + jnp.log1p(jnp.exp(-jnp.abs(v)))


def permuted(order, x):
    rows = x.shape[0]
    stored = lax.broadcasted_iota(jnp.int32, (rows, rows), 0)
    pick = jnp.where(stored == order, 1.0, 0.0).T.astype(jnp.bfloat16)
    high, rest = split(x)
    rest = x - high.astype(jnp.float32)
    mid, low = split(rest)

    def one(part):
        return jnp.dot(pick, part, preferred_element_type=jnp.float32)

    return one(high) + (one(mid) + one(low))


def kernel(
    n, layers,
    p_hbm, z_hbm, q_hbm, u_hbm, w_hbm, b_hbm, qb_hbm, ub_hbm, pb_hbm, order_hbm,
    p_out, z_out, q_out, u_out, w_out, b_out,
    p_ref, z_ref, q_ref, u_ref, w_ref, b_ref, qb_ref, ub_ref, pb_ref, order_ref,
    p_all, z_all, coupling, p_next, own_coupling, w_hi, w_lo, p_hi, p_lo, pt_hi, pt_lo, target0, t_hi, t_lo, change,
    z_right, z_left, z_recv, p_right, p_left, p_recv, layer_send, layer_recv, loads,
):
    rows, width = p_ref.shape
    total = rows * n
    me, layer = lax.axis_index("dp"), lax.axis_index("layer")
    scale = step_weight / total
    has_left, has_right = me > 0, me < n - 1
    has_below, has_above = layer > 0, layer < layers - 1

    barrier = pltpu.get_barrier_semaphore()
    for there, axis, index in (
        (has_left, "dp", me - 1), (has_right, "dp", me + 1),
        (has_below, "layer", layer - 1), (has_above, "layer", layer + 1),
    ):
        @pl.when(there)
        def _():
            pl.semaphore_signal(barrier, inc=1, device_id={axis: index}, device_id_type=MESH)

    load = {}
    for i, (name, source, target) in enumerate((
        ("z", z_hbm, z_ref), ("u", u_hbm, u_ref), ("q", q_hbm, q_ref), ("w", w_hbm, w_ref), ("p", p_hbm, p_ref),
        ("b", b_hbm, b_ref), ("order", order_hbm, order_ref), ("ub", ub_hbm, ub_ref), ("qb", qb_hbm, qb_ref),
        ("pb", pb_hbm, pb_ref),
    )):
        load[name] = pltpu.make_async_copy(source, target, loads.at[i])
        load[name].start()
    load["z"].wait()
    ends = [jnp.where(there, 1, 0) for there in (has_left, has_right, has_below, has_above)]
    pl.semaphore_wait(barrier, ends[0] + ends[1] + ends[2] + ends[3])

    def z_copy(owner, to_right, own=False):
        return pltpu.make_async_remote_copy(
            src_ref=z_ref if own else z_all.at[owner], dst_ref=z_all.at[owner],
            send_sem=(z_right if to_right else z_left).at[owner], recv_sem=z_recv.at[owner],
            device_id={"dp": me + 1 if to_right else me - 1}, device_id_type=MESH,
        )

    def p_copy(owner, to_right):
        return pltpu.make_async_remote_copy(
            src_ref=p_all.at[owner], dst_ref=p_all.at[owner],
            send_sem=(p_right if to_right else p_left).at[owner], recv_sem=p_recv.at[owner],
            device_id={"dp": me + 1 if to_right else me - 1}, device_id_type=MESH,
        )

    up = pltpu.make_async_remote_copy(
        src_ref=own_coupling, dst_ref=coupling, send_sem=layer_send.at[0], recv_sem=layer_recv.at[0],
        device_id={"layer": layer + 1}, device_id_type=MESH,
    )
    down = pltpu.make_async_remote_copy(
        src_ref=p_all.at[me], dst_ref=p_next, send_sem=layer_send.at[1], recv_sem=layer_recv.at[1],
        device_id={"layer": layer - 1}, device_id_type=MESH,
    )

    pl.when(has_right)(lambda: z_copy(me, True, True).start())
    pl.when(has_left)(lambda: z_copy(me, False, True).start())
    load["u"].wait()
    load["q"].wait()
    own_coupling[...] = u_ref[...] - q_ref[...]
    pl.when(has_above)(lambda: up.start())

    for name in ("w", "p", "b", "order", "ub", "qb", "pb"):
        load[name].wait()
    w_hi[...], w_lo[...] = split(w_ref[...])
    weight = (w_hi[...], w_lo[...])
    p, z, bias = p_ref[...], z_ref[...], b_ref[...]
    residual = dot3(split(p), weight) + bias - z
    back = dot3(split(residual), weight, NT)

    @pl.when(jnp.logical_not(has_below))
    def _():
        coupling[...] = permuted(order_ref[...], ub_ref[...] - qb_ref[...])

    pl.when(has_below)(lambda: up.wait_recv())
    p = p - step_input * (back + (coupling[...] + p))
    p_all[me] = p
    p_out[...] = p
    pl.when(has_right)(lambda: p_copy(me, True).start())
    pl.when(has_left)(lambda: p_copy(me, False).start())
    pl.when(has_below)(lambda: down.start())

    @pl.when(jnp.logical_not(has_above))
    def _():
        p_next[...] = permuted(order_ref[...], pb_ref[...])

    pt_hi[pl.ds(width, 16), :] = jnp.ones((16, total), jnp.bfloat16)
    pt_lo[pl.ds(width, 16), :] = jnp.zeros((16, total), jnp.bfloat16)

    def block(owner):
        return pl.ds(pl.multiple_of(owner * rows, rows), rows)

    def take_p(owner, value, z_value=None):
        high, low = split(value)
        p_hi[block(owner), :], p_lo[block(owner), :] = high, low
        across = split(value.T)
        pt_hi[pl.ds(0, width), block(owner)] = across[0]
        pt_lo[pl.ds(0, width), block(owner)] = across[1]
        product = dot3((high, low), (w_hi[...], w_lo[...])) + b_ref[...]
        target0[block(owner), :] = product if z_value is None else product - z_value

    def relay(s, copy):
        @pl.when(me >= s)
        def _():
            copy(me - s, True).wait_recv()
            pl.when(has_right)(lambda: copy(me - s, True).start())

        @pl.when(me + s < n)
        def _():
            copy(me + s, False).wait_recv()
            pl.when(has_left)(lambda: copy(me + s, False).start())

    def use(s, step):
        pl.when(me >= s)(lambda: step(me - s))
        pl.when(me + s < n)(lambda: step(me + s))

    take_p(me, p, z)
    for s in range(1, n):
        relay(s, p_copy)
        if s < n - 1:
            relay(s, z_copy)
        use(s, lambda owner: take_p(owner, p_all[owner], z_all[owner] if s < n - 1 else None))

    stacked = (p_hi[...], p_lo[...])
    moment = scale * (dot3(stacked, stacked, NT) + 1.0)
    moment_parts = split(moment)
    same = lax.broadcasted_iota(jnp.int32, (total, total), 0) == lax.broadcasted_iota(jnp.int32, (total, total), 1)
    steps = jnp.where(same, 3.0, 0.0) - 3.0 * moment + dot3(moment_parts, moment_parts)
    t = scale * dot3((pt_hi[...], pt_lo[...]), split(steps))
    t_hi[...], t_lo[...] = split(t)
    change[...] = dot3((t_hi[...], t_lo[...]), split(target0[...]))

    def add(owner):
        change[...] -= dot3((t_hi[:, block(owner)], t_lo[:, block(owner)]), split(z_all[owner]))

    if n > 1:
        relay(n - 1, z_copy)
        use(n - 1, add)

    w = w_ref[...] - change[pl.ds(0, width), :]
    bias = b_ref[...] - change[pl.ds(width, 1), :]
    w_out[...] = w
    b_out[...] = bias
    target = dot3(split(p_all[me]), split(w)) + bias
    z, q, u = z_ref[...], q_ref[...], u_ref[...]
    z = z - step_preact * ((z - target) + (softplus(z) - q) * jax.nn.sigmoid(z))
    z_out[...] = z
    pl.when(has_above)(lambda: down.wait_recv())
    after = p_next[...]
    q = (penalty_nu * softplus(z) + u + penalty_rho * after) / (penalty_nu + penalty_rho)
    q_out[...] = q
    u_out[...] = u + penalty_rho * (after - q)

    for owner in range(n):
        @pl.when(jnp.logical_and(me >= owner, has_right))
        def _():
            z_copy(owner, True).wait_send()
            p_copy(owner, True).wait_send()
        @pl.when(jnp.logical_and(me <= owner, has_left))
        def _():
            z_copy(owner, False).wait_send()
            p_copy(owner, False).wait_send()
    pl.when(has_above)(lambda: up.wait_send())
    pl.when(has_below)(lambda: down.wait_send())


def store_kernel(*refs):
    sources, targets, sems = refs[:6], refs[6:12], refs[12]
    copies = [pltpu.make_async_copy(a, b, sems.at[i]) for i, (a, b) in enumerate(zip(sources, targets))]
    for copy in copies:
        copy.start()
    for copy in copies:
        copy.wait()


def gathered_body(n, layers, layer_inputs, pre_acts, layer_outputs, multipliers, weights, biases, prev_outputs, prev_multipliers, next_inputs, row_order):
    rows, width = prev_outputs.shape
    total = rows * n
    f32, b16 = jnp.float32, jnp.bfloat16
    dma = pltpu.SemaphoreType.DMA
    block = jax.ShapeDtypeStruct((rows, width), f32)
    hbm = pl.BlockSpec(memory_space=pltpu.HBM)
    shapes = (block,) * 4 + (jax.ShapeDtypeStruct((width, width), f32), jax.ShapeDtypeStruct((1, width), f32))
    vm = pl.BlockSpec(memory_space=pltpu.VMEM)
    kept = (sum(x.size for x in shapes) * 4 + 2**14) // 2**12 * 2**12
    outs = pl.pallas_call(
        functools.partial(kernel, n, layers),
        out_shape=tuple(pltpu.VMEM(x.shape, x.dtype) for x in shapes),
        in_specs=[hbm] * 10,
        out_specs=(vm,) * 6,
        scratch_shapes=[
            *(pltpu.VMEM((rows, width), f32),) * 4,
            pltpu.VMEM((width, width), f32), pltpu.VMEM((1, width), f32),
            *(pltpu.VMEM((rows, width), f32),) * 3,
            pltpu.VMEM((1, rows), jnp.int32),
            pltpu.VMEM((n, rows, width), f32), pltpu.VMEM((n, rows, width), f32),
            pltpu.VMEM((rows, width), f32), pltpu.VMEM((rows, width), f32), pltpu.VMEM((rows, width), f32),
            pltpu.VMEM((width, width), b16), pltpu.VMEM((width, width), b16),
            pltpu.VMEM((total, width), b16), pltpu.VMEM((total, width), b16),
            pltpu.VMEM((width + 16, total), b16), pltpu.VMEM((width + 16, total), b16),
            pltpu.VMEM((total, width), f32),
            pltpu.VMEM((width + 16, total), b16), pltpu.VMEM((width + 16, total), b16),
            pltpu.VMEM((width + 16, width), f32),
            dma((n,)), dma((n,)), dma((n,)), dma((n,)), dma((n,)), dma((n,)), dma((2,)), dma((2,)), dma((10,)),
        ],
        compiler_params=pltpu.CompilerParams(collective_id=0, has_side_effects=True, vmem_limit_bytes=VMEM_BYTES - kept),
    )(layer_inputs[0], pre_acts[0], layer_outputs[0], multipliers[0], weights[0], biases, prev_outputs, prev_multipliers, next_inputs, row_order)
    outs = pl.pallas_call(
        store_kernel, out_shape=shapes, in_specs=[vm] * 6, out_specs=(hbm,) * 6,
        scratch_shapes=[dma((6,))], compiler_params=pltpu.CompilerParams(vmem_limit_bytes=2**20),
    )(*outs)
    return tuple(x[None] for x in outs[:5]) + (outs[5],)


def solution(mesh):
    n, layers = mesh.shape["dp"], mesh.shape["layer"]
    body = functools.partial(gathered_body, n, layers) if n <= 8 else summed_body
    return jax.shard_map(
        body,
        mesh=mesh,
        in_specs=(
            P("layer", ("groups", "dp"), None),
            P("layer", ("groups", "dp"), None),
            P("layer", ("groups", "dp"), None),
            P("layer", ("groups", "dp"), None),
            P(("groups", "layer"), None, None),
            P(("groups", "layer"), None),
            P(("groups", "dp"), None),
            P(("groups", "dp"), None),
            P(("groups", "dp"), None),
            P(("groups", "dp"), None),
        ),
        out_specs=(
            P("layer", ("groups", "dp"), None),
            P("layer", ("groups", "dp"), None),
            P("layer", ("groups", "dp"), None),
            P("layer", ("groups", "dp"), None),
            P(("groups", "layer"), None, None),
            P(("groups", "layer"), None),
        ),
        check_vma=False,
    )
```

```python
import functools

import jax
import jax.numpy as jnp
from jax import lax
from jax.experimental import pallas as pl
from jax.experimental.pallas import tpu as pltpu
from jax.sharding import PartitionSpec as P

INNER = 3


penalty_nu = 1.0
penalty_rho = 1.0
step_input = 0.2
step_weight = 0.3
step_preact = 0.5


def from_behind(x, axis, by):
    count = lax.axis_size(axis)
    pairs = [(i, i + by) for i in range(count) if 0 <= i + by < count]
    return lax.ppermute(x, axis, pairs)


def matmul(left, right):
    return jnp.dot(left, right, precision=lax.Precision.HIGHEST)


def summed_body(
    layer_inputs,
    pre_acts,
    layer_outputs,
    multipliers,
    weights,
    biases,
    prev_outputs,
    prev_multipliers,
    next_inputs,
    row_order,
):
    row_perm = row_order[0]
    edge_outputs = jnp.take(prev_outputs, row_perm, axis=0)
    edge_duals = jnp.take(prev_multipliers, row_perm, axis=0)
    edge_inputs = jnp.take(next_inputs, row_perm, axis=0)
    first_layer = lax.axis_index("layer") == 0
    last_layer = lax.axis_index("layer") == lax.axis_size("layer") - 1
    row_count = layer_inputs.shape[1] * lax.axis_size("dp")
    scale = step_weight / row_count
    inputs, preact, outputs, duals = (
        layer_inputs[0],
        pre_acts[0],
        layer_outputs[0],
        multipliers[0],
    )
    weight, offset = (weights[0], biases[0])
    before_out, before_dual = from_behind((outputs, duals), "layer", 1)
    before_out = jnp.where(first_layer, edge_outputs, before_out)
    before_dual = jnp.where(first_layer, edge_duals, before_dual)
    coupling = before_dual + penalty_rho * (inputs - before_out)
    residual = matmul(inputs, weight) + offset[None, :] - preact
    inputs = inputs - step_input * (penalty_nu * matmul(residual, weight.T) + coupling)
    gram_matrix, cross_term, column_sums, preact_sums = lax.psum(
        (
            matmul(inputs.T, inputs),
            matmul(inputs.T, preact),
            jnp.sum(inputs, axis=0),
            jnp.sum(preact, axis=0),
        ),
        "dp",
    )
    for inner_step in range(INNER):
        grad_weight = (
            matmul(gram_matrix, weight) + column_sums[:, None] * offset[None, :] - cross_term
        )
        grad_offset = matmul(column_sums[None, :], weight)[0] + row_count * offset - preact_sums
        weight = weight - scale * grad_weight
        offset = offset - scale * grad_offset
    target = matmul(inputs, weight) + offset[None, :]
    preact = preact - step_preact * (
        preact - target + (jax.nn.softplus(preact) - outputs) * jax.nn.sigmoid(preact)
    )
    after_in = from_behind(inputs, "layer", -1)
    after_in = jnp.where(last_layer, edge_inputs, after_in)
    outputs = (penalty_nu * jax.nn.softplus(preact) + duals + penalty_rho * after_in) / (
        penalty_nu + penalty_rho
    )
    duals = duals + penalty_rho * (after_in - outputs)
    return (inputs[None], preact[None], outputs[None], duals[None], weight[None], offset[None])


MESH = pl.DeviceIdType.MESH
VMEM_BYTES = 67043328
NN = (((1,), (0,)), ((), ()))
NT = (((1,), (1,)), ((), ()))


def split(x):
    high = x.astype(jnp.bfloat16)
    return high, (x - high.astype(jnp.float32)).astype(jnp.bfloat16)


def dot3(left, right, dims=NN):
    def one(a, b):
        return lax.dot_general(a, b, dims, preferred_element_type=jnp.float32)

    return one(left[0], right[0]) + (one(left[0], right[1]) + one(left[1], right[0]))


def softplus(v):
    return jnp.maximum(v, 0.0) + jnp.log1p(jnp.exp(-jnp.abs(v)))


def permuted(order, x):
    rows = x.shape[0]
    stored = lax.broadcasted_iota(jnp.int32, (rows, rows), 0)
    pick = jnp.where(stored == order, 1.0, 0.0).T.astype(jnp.bfloat16)
    high, rest = split(x)
    rest = x - high.astype(jnp.float32)
    mid, low = split(rest)

    def one(part):
        return jnp.dot(pick, part, preferred_element_type=jnp.float32)

    return one(high) + (one(mid) + one(low))


def kernel(
    n, layers,
    p_hbm, z_hbm, q_hbm, u_hbm, w_hbm, b_hbm, qb_hbm, ub_hbm, pb_hbm, order_hbm,
    p_out, z_out, q_out, u_out, w_out, b_out,
    p_ref, z_ref, q_ref, u_ref, w_ref, b_ref, qb_ref, ub_ref, pb_ref, order_ref,
    p_all, z_all, coupling, p_next, own_coupling, w_hi, w_lo, p_hi, p_lo, pt_hi, pt_lo, target0, t_hi, t_lo, change,
    z_right, z_left, z_recv, p_right, p_left, p_recv, layer_send, layer_recv, loads, products,
):
    rows, width = p_ref.shape
    total = rows * n
    me, layer = lax.axis_index("dp"), lax.axis_index("layer")
    scale = step_weight / total
    has_left, has_right = me > 0, me < n - 1
    has_below, has_above = layer > 0, layer < layers - 1

    barrier = pltpu.get_barrier_semaphore()
    for there, axis, index in (
        (has_left, "dp", me - 1), (has_right, "dp", me + 1),
        (has_below, "layer", layer - 1), (has_above, "layer", layer + 1),
    ):
        @pl.when(there)
        def _():
            pl.semaphore_signal(barrier, inc=1, device_id={axis: index}, device_id_type=MESH)

    load = {}
    for i, (name, source, target) in enumerate((
        ("z", z_hbm, z_ref), ("u", u_hbm, u_ref), ("q", q_hbm, q_ref), ("w", w_hbm, w_ref), ("p", p_hbm, p_ref),
        ("b", b_hbm, b_ref), ("order", order_hbm, order_ref), ("ub", ub_hbm, ub_ref), ("qb", qb_hbm, qb_ref),
        ("pb", pb_hbm, pb_ref),
    )):
        load[name] = pltpu.make_async_copy(source, target, loads.at[i])
        load[name].start()
    load["z"].wait()
    ends = [jnp.where(there, 1, 0) for there in (has_left, has_right, has_below, has_above)]
    pl.semaphore_wait(barrier, ends[0] + ends[1] + ends[2] + ends[3])

    def z_copy(owner, to_right, own=False):
        return pltpu.make_async_remote_copy(
            src_ref=z_ref if own else z_all.at[owner], dst_ref=z_all.at[owner],
            send_sem=(z_right if to_right else z_left).at[owner], recv_sem=z_recv.at[owner],
            device_id={"dp": me + 1 if to_right else me - 1}, device_id_type=MESH,
        )

    def p_copy(owner, to_right):
        return pltpu.make_async_remote_copy(
            src_ref=p_all.at[owner], dst_ref=p_all.at[owner],
            send_sem=(p_right if to_right else p_left).at[owner], recv_sem=p_recv.at[owner],
            device_id={"dp": me + 1 if to_right else me - 1}, device_id_type=MESH,
        )

    up = pltpu.make_async_remote_copy(
        src_ref=own_coupling, dst_ref=coupling, send_sem=layer_send.at[0], recv_sem=layer_recv.at[0],
        device_id={"layer": layer + 1}, device_id_type=MESH,
    )
    down = pltpu.make_async_remote_copy(
        src_ref=p_all.at[me], dst_ref=p_next, send_sem=layer_send.at[1], recv_sem=layer_recv.at[1],
        device_id={"layer": layer - 1}, device_id_type=MESH,
    )

    pl.when(has_right)(lambda: z_copy(me, True, True).start())
    pl.when(has_left)(lambda: z_copy(me, False, True).start())
    load["u"].wait()
    load["q"].wait()
    own_coupling[...] = u_ref[...] - q_ref[...]
    pl.when(has_above)(lambda: up.start())

    for name in ("w", "p", "b", "order", "ub", "qb", "pb"):
        load[name].wait()
    w_hi[...], w_lo[...] = split(w_ref[...])
    weight = (w_hi[...], w_lo[...])
    p, z, bias = p_ref[...], z_ref[...], b_ref[...]
    residual = dot3(split(p), weight) + bias - z
    back = dot3(split(residual), weight, NT)

    @pl.when(jnp.logical_not(has_below))
    def _():
        coupling[...] = permuted(order_ref[...], ub_ref[...] - qb_ref[...])

    pl.when(has_below)(lambda: up.wait_recv())
    p = p - step_input * (back + (coupling[...] + p))
    p_all[me] = p
    p_out[...] = p
    pl.when(has_right)(lambda: p_copy(me, True).start())
    pl.when(has_left)(lambda: p_copy(me, False).start())
    pl.when(has_below)(lambda: down.start())

    @pl.when(jnp.logical_not(has_above))
    def _():
        p_next[...] = permuted(order_ref[...], pb_ref[...])

    pt_hi[pl.ds(width, 16), :] = jnp.ones((16, total), jnp.bfloat16)
    pt_lo[pl.ds(width, 16), :] = jnp.zeros((16, total), jnp.bfloat16)

    def block(owner):
        return pl.ds(pl.multiple_of(owner * rows, rows), rows)

    p_hi[...] = jnp.zeros((total, width), jnp.bfloat16)
    p_lo[...] = jnp.zeros((total, width), jnp.bfloat16)

    def take_p(owner, value, z_value=None):
        high, low = split(value)
        p_hi[block(owner), :], p_lo[block(owner), :] = high, low
        stacked = (p_hi[...], p_lo[...])
        products[block(owner), :] = dot3((high, low), stacked, NT)
        products[:, block(owner)] = dot3(stacked, (high, low), NT)
        across = split(value.T)
        pt_hi[pl.ds(0, width), block(owner)] = across[0]
        pt_lo[pl.ds(0, width), block(owner)] = across[1]
        product = dot3((high, low), (w_hi[...], w_lo[...])) + b_ref[...]
        target0[block(owner), :] = product if z_value is None else product - z_value

    def relay(s, copy):
        @pl.when(me >= s)
        def _():
            copy(me - s, True).wait_recv()
            pl.when(has_right)(lambda: copy(me - s, True).start())

        @pl.when(me + s < n)
        def _():
            copy(me + s, False).wait_recv()
            pl.when(has_left)(lambda: copy(me + s, False).start())

    def use(s, step):
        pl.when(me >= s)(lambda: step(me - s))
        pl.when(me + s < n)(lambda: step(me + s))

    take_p(me, p, z)
    for s in range(1, n):
        relay(s, p_copy)
        if s < n - 1:
            relay(s, z_copy)
        use(s, lambda owner: take_p(owner, p_all[owner], z_all[owner] if s < n - 1 else None))

    moment = scale * (products[...] + 1.0)
    moment_parts = split(moment)
    same = lax.broadcasted_iota(jnp.int32, (total, total), 0) == lax.broadcasted_iota(jnp.int32, (total, total), 1)
    steps = jnp.where(same, 3.0, 0.0) - 3.0 * moment + dot3(moment_parts, moment_parts)
    t = scale * dot3((pt_hi[...], pt_lo[...]), split(steps))
    t_hi[...], t_lo[...] = split(t)
    change[...] = dot3((t_hi[...], t_lo[...]), split(target0[...]))

    def add(owner):
        change[...] -= dot3((t_hi[:, block(owner)], t_lo[:, block(owner)]), split(z_all[owner]))

    if n > 1:
        relay(n - 1, z_copy)
        use(n - 1, add)

    w = w_ref[...] - change[pl.ds(0, width), :]
    bias = b_ref[...] - change[pl.ds(width, 1), :]
    w_out[...] = w
    b_out[...] = bias
    target = dot3(split(p_all[me]), split(w)) + bias
    z, q, u = z_ref[...], q_ref[...], u_ref[...]
    z = z - step_preact * ((z - target) + (softplus(z) - q) * jax.nn.sigmoid(z))
    z_out[...] = z
    pl.when(has_above)(lambda: down.wait_recv())
    after = p_next[...]
    q = (penalty_nu * softplus(z) + u + penalty_rho * after) / (penalty_nu + penalty_rho)
    q_out[...] = q
    u_out[...] = u + penalty_rho * (after - q)

    for owner in range(n):
        @pl.when(jnp.logical_and(me >= owner, has_right))
        def _():
            z_copy(owner, True).wait_send()
            p_copy(owner, True).wait_send()
        @pl.when(jnp.logical_and(me <= owner, has_left))
        def _():
            z_copy(owner, False).wait_send()
            p_copy(owner, False).wait_send()
    pl.when(has_above)(lambda: up.wait_send())
    pl.when(has_below)(lambda: down.wait_send())


def store_kernel(*refs):
    sources, targets, sems = refs[:6], refs[6:12], refs[12]
    copies = [pltpu.make_async_copy(a, b, sems.at[i]) for i, (a, b) in enumerate(zip(sources, targets))]
    for copy in copies:
        copy.start()
    for copy in copies:
        copy.wait()


def gathered_body(n, layers, layer_inputs, pre_acts, layer_outputs, multipliers, weights, biases, prev_outputs, prev_multipliers, next_inputs, row_order):
    rows, width = prev_outputs.shape
    total = rows * n
    f32, b16 = jnp.float32, jnp.bfloat16
    dma = pltpu.SemaphoreType.DMA
    block = jax.ShapeDtypeStruct((rows, width), f32)
    hbm = pl.BlockSpec(memory_space=pltpu.HBM)
    shapes = (block,) * 4 + (jax.ShapeDtypeStruct((width, width), f32), jax.ShapeDtypeStruct((1, width), f32))
    vm = pl.BlockSpec(memory_space=pltpu.VMEM)
    kept = (sum(x.size for x in shapes) * 4 + 2**14) // 2**12 * 2**12
    outs = pl.pallas_call(
        functools.partial(kernel, n, layers),
        out_shape=tuple(pltpu.VMEM(x.shape, x.dtype) for x in shapes),
        in_specs=[hbm] * 10,
        out_specs=(vm,) * 6,
        scratch_shapes=[
            *(pltpu.VMEM((rows, width), f32),) * 4,
            pltpu.VMEM((width, width), f32), pltpu.VMEM((1, width), f32),
            *(pltpu.VMEM((rows, width), f32),) * 3,
            pltpu.VMEM((1, rows), jnp.int32),
            pltpu.VMEM((n, rows, width), f32), pltpu.VMEM((n, rows, width), f32),
            pltpu.VMEM((rows, width), f32), pltpu.VMEM((rows, width), f32), pltpu.VMEM((rows, width), f32),
            pltpu.VMEM((width, width), b16), pltpu.VMEM((width, width), b16),
            pltpu.VMEM((total, width), b16), pltpu.VMEM((total, width), b16),
            pltpu.VMEM((width + 16, total), b16), pltpu.VMEM((width + 16, total), b16),
            pltpu.VMEM((total, width), f32),
            pltpu.VMEM((width + 16, total), b16), pltpu.VMEM((width + 16, total), b16),
            pltpu.VMEM((width + 16, width), f32),
            dma((n,)), dma((n,)), dma((n,)), dma((n,)), dma((n,)), dma((n,)), dma((2,)), dma((2,)), dma((10,)), pltpu.VMEM((total, total), f32),
        ],
        compiler_params=pltpu.CompilerParams(collective_id=0, has_side_effects=True, vmem_limit_bytes=VMEM_BYTES - kept),
    )(layer_inputs[0], pre_acts[0], layer_outputs[0], multipliers[0], weights[0], biases, prev_outputs, prev_multipliers, next_inputs, row_order)
    outs = pl.pallas_call(
        store_kernel, out_shape=shapes, in_specs=[vm] * 6, out_specs=(hbm,) * 6,
        scratch_shapes=[dma((6,))], compiler_params=pltpu.CompilerParams(vmem_limit_bytes=2**20),
    )(*outs)
    return tuple(x[None] for x in outs[:5]) + (outs[5],)


def solution(mesh):
    n, layers = mesh.shape["dp"], mesh.shape["layer"]
    body = functools.partial(gathered_body, n, layers) if n <= 8 else summed_body
    return jax.shard_map(
        body,
        mesh=mesh,
        in_specs=(
            P("layer", ("groups", "dp"), None),
            P("layer", ("groups", "dp"), None),
            P("layer", ("groups", "dp"), None),
            P("layer", ("groups", "dp"), None),
            P(("groups", "layer"), None, None),
            P(("groups", "layer"), None),
            P(("groups", "dp"), None),
            P(("groups", "dp"), None),
            P(("groups", "dp"), None),
            P(("groups", "dp"), None),
        ),
        out_specs=(
            P("layer", ("groups", "dp"), None),
            P("layer", ("groups", "dp"), None),
            P("layer", ("groups", "dp"), None),
            P("layer", ("groups", "dp"), None),
            P(("groups", "layer"), None, None),
            P(("groups", "layer"), None),
        ),
        check_vma=False,
    )
```
